128 devices in a mesh: dom: 32 (over z, x, core), blk: 4 (over y).
Axes of the slice: x: 4, y: 4, z: 4, core: 2. Of those that a mesh axis runs over, the one named last changes fastest.
Arguments:
- displacement: float32 [16384, 96], P(('dom', 'blk')), may hold values from -6 to 6
- damage: float32 [16384, 96], P(('dom', 'blk')), may hold values from 0 to 0.95
- applied_load: float32 [16384, 96], P(('dom', 'blk')), may hold values from -300 to 300
- tangent: bfloat16 [16384, 5, 96, 96], P(('dom', 'blk')), may hold values from -0.625 to 0.625
- laplacian: bfloat16 [16384, 5, 96, 96], P(('dom', 'blk')), may hold values from -0.25 to 0.25
- block_columns: int32 [16384, 5], P(('dom', 'blk')), may hold values from 0 to 1023, as said below
- send_lists: int32 [32, 2, 256], P('dom'), may hold values from -1 to 511, as said below
- hist_mech: float32 [16384, 27, 96], P(('dom', 'blk')), may hold values from 0 to 200
- mech_dest: int32 [16384], P(('dom', 'blk')), may hold values from 0 to 16383, as said below
- strain_matrix: float32 [27, 96, 96], replicated, may hold values from -0.625 to 0.625
- quad_weight: float32 [27], replicated, may hold values from 0.018518519 to 0.055555556
Outputs:
- mech_out: float32 [16384, 96], P(('dom', 'blk'))
- dmg_out: float32 [16384, 96], P(('dom', 'blk'))
- norms: float32 [2], replicated
The draws below stay inside these ranges and needn't reach their ends.
Inputs may be any that keep to these rules, and one draw needn't show every extreme that they name: mech_dest is a permutation of the block rows. The 128 rows of one device go to at most 2 rows of any one device (itself included), and that many are reached in every draw. `send_lists`: -1 marks an unused slot; used slots come first and name distinct rows of the group, numbered within the group. Group 0 lists nothing for the group below and the last group nothing for the group above. Some list uses all 256 slots. `block_columns`: entries of the ghost parts of the extended numbering name only used slots of the neighbours' lists, never those of a missing neighbour, and every used slot is named by some block row of the receiving group.
All inputs are finite; a program needn't handle non-finite values.
Results may differ from the reference program's by a relative error of at most 0.00047.
Values may be sent and summed in bfloat16 or wider, within the bound.
A program may use at most 128 MiB of HBM per device.

```python
import math
import jax
import jax.numpy as jnp
from jax import lax

BLOCK = 96
KBLK = 5
QUAD = 27
RDEV = 128
RGRP = 512
GMAX = 256
NBR = 16384
N_DOM = 32
DEVICES = 128


def perm_slots(sub_key):
    return jax.random.permutation(sub_key, RDEV)


def perm_group(sub_key):
    return jax.random.permutation(sub_key, RGRP)


def route_map(key):
    base_count = RDEV // DEVICES
    sub_keys = jax.random.split(jax.random.fold_in(key, 11), 4)
    offsets = jnp.arange(DEVICES)
    coins = jax.random.randint(sub_keys[0], (DEVICES,), 0, 2)
    chosen = jax.random.randint(sub_keys[1], (), 0, DEVICES)
    coins = jnp.where(offsets == chosen, 1, coins)
    coins = jnp.where(offsets == (chosen + 1) % DEVICES, 0, coins)
    counts = base_count + coins - jnp.roll(coins, -1)
    bounds = jnp.cumsum(counts)
    offset_of = jnp.searchsorted(bounds, jnp.arange(RDEV), side='right').astype(jnp.int32)
    shuffle = jax.random.permutation(sub_keys[2], RDEV)
    shift = jnp.zeros((RDEV,), jnp.int32).at[shuffle].set(offset_of)
    slot_perm = jax.vmap(perm_slots)(jax.random.split(sub_keys[3], DEVICES))
    sources = jnp.arange(DEVICES)[:, None]
    slot_ids = jnp.arange(RDEV)[None, :]
    target = (sources + shift[None, :]) % DEVICES
    dest = target * RDEV + slot_perm[target, slot_ids]
    return dest.reshape(-1).astype(jnp.int32)


def draw_mech_dest(key, part):
    return route_map(key)


def draw_hist_mech(key, part):
    dest = route_map(key)
    trend_pos = dest.astype(jnp.float32) / max(NBR - 1, 1)
    sub_keys = jax.random.split(jax.random.fold_in(key, 23), 2)
    row_scale = jnp.exp(jax.random.uniform(sub_keys[0], (NBR, 1, 1)) * math.log(10.0))
    values = jnp.exp(jax.random.uniform(sub_keys[1], (NBR, QUAD, BLOCK), minval=-3.0, maxval=0.7))
    trend = 1.0 + 2.0 * trend_pos
    return (values * row_scale * trend[:, None, None]).astype(jnp.float32)


def draw_applied_load(key, part):
    sub_keys = jax.random.split(jax.random.fold_in(key, 29), 3)
    trend_pos = jnp.arange(NBR).astype(jnp.float32) / max(NBR - 1, 1)
    row_scale = jnp.exp(jax.random.uniform(sub_keys[0], (NBR, 1)) * math.log(10.0))
    column_scale = jnp.exp(jax.random.uniform(sub_keys[1], (1, BLOCK)) * math.log(10.0))
    values = jax.random.truncated_normal(sub_keys[2], -6.0, 6.0, (NBR, BLOCK))
    trend = 1.0 + 2.0 * trend_pos
    return (0.1 * values * row_scale * column_scale * trend[:, None]).astype(jnp.float32)


def ghost_plan(key):
    sub_keys = jax.random.split(jax.random.fold_in(key, 37), 6)
    counts = jax.random.randint(sub_keys[0], (N_DOM, 2), GMAX // 4, GMAX + 1)
    chosen = jax.random.randint(sub_keys[1], (), 0, N_DOM - 1)
    group_ids = jnp.arange(N_DOM)
    counts = counts.at[:, 1].set(jnp.where(group_ids == chosen, GMAX, counts[:, 1]))
    counts = counts.at[0, 0].set(0).at[N_DOM - 1, 1].set(0)
    orders = jax.vmap(perm_group)(jax.random.split(sub_keys[2], N_DOM * 2)).reshape(N_DOM, 2, RGRP)[:, :, :GMAX]
    listed = jnp.where(jnp.arange(GMAX)[None, None, :] < counts[:, :, None], orders, -1)
    zero_one = jnp.zeros((1,), counts.dtype)
    below = jnp.concatenate([zero_one, counts[:-1, 1]])
    above = jnp.concatenate([counts[1:, 0], zero_one])
    mixers = jax.vmap(perm_group)(jax.random.split(sub_keys[3], N_DOM))
    spread = jax.random.randint(sub_keys[4], (N_DOM, RGRP, KBLK), 0, RGRP)
    own_index = jnp.broadcast_to(jnp.arange(RGRP)[None, :], (N_DOM, RGRP))
    low_col = jnp.where(below[:, None] > 0, RGRP + mixers % jnp.maximum(below[:, None], 1), spread[:, :, 1])
    high_col = jnp.where(above[:, None] > 0, RGRP + GMAX + mixers % jnp.maximum(above[:, None], 1), spread[:, :, 2])
    entries = jnp.concatenate([own_index[:, :, None], low_col[:, :, None], high_col[:, :, None], spread[:, :, 3:]], axis=2)
    scores = jax.random.randint(sub_keys[5], (N_DOM, RGRP, KBLK), 0, 1 << 20) * KBLK + jnp.arange(KBLK)[None, None, :]
    order_k = jnp.argsort(scores, axis=2)
    columns = jnp.take_along_axis(entries, order_k, axis=2)
    return (listed.astype(jnp.int32), columns.reshape(NBR, KBLK).astype(jnp.int32))


def draw_send_lists(key, part):
    return ghost_plan(key)[0]


def draw_block_columns(key, part):
    return ghost_plan(key)[1]


def level_of(rng, shape, shards, smallest, high):
    def one(dim, shards_of):
        heights = jax.random.uniform(jax.random.fold_in(jax.random.fold_in(rng, 6), dim), (shards_of,), jnp.float32, smallest / len(shards), high / len(shards))
        return jnp.repeat(jnp.exp(heights), shape[dim] // shards_of).reshape((-1,) + (1,) * (len(shape) - dim - 1))

    loudness = one(*shards[0])
    for cut in shards[1:]:
        loudness = loudness * one(*cut)
    return loudness


def gaussian(key, dims, scale, most, cuts=(), held_as=jnp.bfloat16):
    array = jax.random.normal(key, dims, jnp.float32) * scale
    if len(cuts) > 0:
        array = level_of(key, dims, cuts, -0.22, 0.18) * array
    return jnp.clip(array, min=-most, max=most).astype(held_as)


def setup_inputs(seed: int = 0) -> dict:
    splits = jax.random.split(jax.random.key(seed), 12)
    return {
        "displacement": gaussian(splits[0], (NBR, BLOCK), 1.0, 6.0, ((0, 128),), jnp.float32),
        "damage": jnp.clip(0.95 * jax.random.uniform(splits[1], (NBR, BLOCK), jnp.float32) ** level_of(splits[1], (NBR, BLOCK), ((0, 128),), -0.2, 0.2), 0.0, 0.95),
        "applied_load": draw_applied_load(jax.random.fold_in(splits[11], 71), 0),
        "tangent": gaussian(splits[3], (NBR, KBLK, BLOCK, BLOCK), BLOCK ** -0.5, 0.625, ((0, 128),)),
        "laplacian": gaussian(splits[4], (NBR, KBLK, BLOCK, BLOCK), (KBLK * BLOCK) ** -0.5, 0.25, ((0, 128),)),
        "block_columns": draw_block_columns(jax.random.fold_in(splits[11], 71), 0),
        "send_lists": draw_send_lists(jax.random.fold_in(splits[11], 71), 0),
        "hist_mech": draw_hist_mech(jax.random.fold_in(splits[11], 71), 0),
        "mech_dest": draw_mech_dest(jax.random.fold_in(splits[11], 71), 0),
        "strain_matrix": gaussian(splits[9], (QUAD, BLOCK, BLOCK), BLOCK ** -0.5, 0.625, (), jnp.float32),
        "quad_weight": jnp.clip(jax.random.uniform(splits[10], (QUAD,), jnp.float32, 0.018518519, 0.055555556), 0.018518519, 0.055555556),
    }


def apply_blocks(packed):
    tan_rows, lap_rows, disp_near, dmg_near = packed
    mech_sum = jnp.einsum('ikrc,ikc->ir', tan_rows.astype(jnp.float32), disp_near.astype(jnp.float32))
    diffuse = jnp.einsum('ikrc,ikc->ir', lap_rows.astype(jnp.float32), dmg_near.astype(jnp.float32))
    return (mech_sum, diffuse)

def reference(displacement, damage, applied_load, tangent, laplacian, block_columns, send_lists, hist_mech, mech_dest, strain_matrix, quad_weight):
    root_deg = jnp.sqrt((1.0 - damage) ** 2 + 0.001)
    fields = jnp.stack([(root_deg * displacement).astype(jnp.bfloat16), damage.astype(jnp.bfloat16)])
    grouped = fields.reshape(2, N_DOM, RGRP, BLOCK)
    listed = send_lists >= 0
    safe_index = jnp.maximum(send_lists, 0).astype(jnp.int32)
    group_index = jnp.arange(N_DOM, dtype=jnp.int32)[:, None, None]
    picked = grouped[:, group_index, safe_index]
    picked = jnp.where(listed[None, :, :, :, None], picked, jnp.zeros((), jnp.bfloat16))
    empty_rows = jnp.zeros((2, 1, GMAX, BLOCK), jnp.bfloat16)
    lower_ghost = jnp.concatenate([empty_rows, picked[:, :-1, 1]], axis=1)
    upper_ghost = jnp.concatenate([picked[:, 1:, 0], empty_rows], axis=1)
    extended = jnp.concatenate([grouped, lower_ghost, upper_ghost], axis=2)
    column_grid = block_columns.reshape(N_DOM, RGRP, KBLK).astype(jnp.int32)
    near_rows = extended[:, group_index, column_grid].reshape(2, NBR, KBLK, BLOCK)
    mech_sum, diffuse = lax.map(apply_blocks, (tangent.reshape(DEVICES, RDEV, KBLK, BLOCK, BLOCK), laplacian.reshape(DEVICES, RDEV, KBLK, BLOCK, BLOCK), near_rows[0].reshape(DEVICES, RDEV, KBLK, BLOCK), near_rows[1].reshape(DEVICES, RDEV, KBLK, BLOCK)))
    mech_sum = mech_sum.reshape(NBR, BLOCK)
    diffuse = diffuse.reshape(NBR, BLOCK)
    mech_res = root_deg * mech_sum - applied_load
    history = jnp.zeros((NBR, QUAD, BLOCK), jnp.float32).at[mech_dest].set(hist_mech)
    strain = jnp.einsum('qcr,ir->iqc', strain_matrix, displacement, precision=lax.Precision.HIGHEST)
    energy = 0.5 * strain * strain
    source = jnp.einsum('q,iqc->ic', quad_weight, jnp.maximum(history, energy), precision=lax.Precision.HIGHEST)
    dmg_res = diffuse + (1.0 + 2.0 * source) * damage - 2.0 * source
    mech_norm = jnp.sqrt(jnp.mean(mech_res * mech_res) + 1e-06)
    dmg_norm = jnp.sqrt(jnp.mean(dmg_res * dmg_res) + 1e-06)
    return (mech_res / mech_norm, dmg_res / dmg_norm, jnp.stack([mech_norm, dmg_norm]))
```

```python
import functools

import jax
import jax.numpy as jnp
from jax import lax
from jax.experimental import pallas as pl
from jax.experimental.pallas import tpu as pltpu
from jax.sharding import PartitionSpec as P

MESH = pl.DeviceIdType.MESH
F32 = jnp.float32
BF16 = jnp.bfloat16
LANES = 128


def dot(a, b):
    return jnp.dot(a, b, preferred_element_type=F32)


def dot_nt(a, b):
    return lax.dot_general(a, b, (((1,), (1,)), ((), ())), preferred_element_type=F32)


def halves(x):
    hi = x.astype(BF16)
    return hi, (x - hi.astype(F32)).astype(BF16)


def as_bf16(mask):
    return jnp.where(mask, 1.0, 0.0).astype(BF16)


def bytes_wait(ref, sem):
    pltpu.make_async_copy(ref, ref, sem).wait()


def block_rows(mat, near, out):
    kblk, width = near.shape[0], near.shape[1]

    def rows(rb, carry):
        r0 = pl.multiple_of(rb * 8, 8)
        acc = None
        for k in range(kblk):
            for c in range(0, width, 16):
                part = mat[k, pl.ds(r0, 8), c : c + 16, :].astype(F32) * near[k, c : c + 16, :][None]
                acc = part if acc is None else acc + part
        out[pl.ds(r0, 8), :] = jnp.sum(acc, axis=1)
        return carry

    lax.fori_loop(0, width // 8, rows, 0)


def kernel(
    nd,
    nb,
    disp_h,
    dmg_h,
    load_h,
    tan_h,
    lap_h,
    cols_h,
    lists_h,
    hist_h,
    dest_h,
    smat_h,
    quad_h,
    mech_o,
    dmg_o,
    norm_o,
    disp,
    dmg,
    load,
    tan,
    lap,
    cols,
    lists,
    hist,
    smat,
    quad,
    dall,
    grp_d,
    grp_w,
    pick_d,
    pick_w,
    ghost_d,
    ghost_w,
    pickhot,
    nearhot,
    near_d,
    near_w,
    s_hi,
    s_lo,
    diffuse,
    mech,
    ohm,
    h2s,
    h2r,
    h3s,
    h3r,
    ld,
    ss,
    rs,
):
    n = nd * nb
    g1 = 2 * nb
    g2 = n // g1
    width, rows = disp.shape
    kblk = cols.shape[0]
    gmax = lists.shape[1]
    shift = rows.bit_length() - 1
    wl = h2s.shape[2] // 2
    dom = lax.axis_index("dom")
    blk = lax.axis_index("blk")
    me = dom * nb + blk
    base = (me // g1) * g1

    def loc(p):
        return (p // nb, lax.rem(p, nb))

    def signal(p):
        pl.semaphore_signal(barrier, inc=1, device_id=loc(p), device_id_type=MESH)

    def send(src, dst, s, r, p):
        pltpu.make_async_remote_copy(
            src_ref=src, dst_ref=dst, send_sem=s, recv_sem=r, device_id=loc(p), device_id_type=MESH
        ).start()

    barrier = pltpu.get_barrier_semaphore()

    @pl.loop(1, g1)
    def _(j):
        signal(base + lax.rem(me + j, g1))

    @pl.loop(1, g2)
    def _(j):
        signal(lax.rem(me + g1 * j, n))

    signal(lax.rem(me + nb, n))
    signal(lax.rem(me + n - nb, n))

    loads = []
    for i, (src, dst) in enumerate(
        (
            (dmg_h, dmg),
            (disp_h, disp),
            (dest_h, dall.at[me]),
            (lists_h, lists),
            (cols_h, cols),
            (lap_h, lap),
            (smat_h, smat),
            (hist_h, hist),
            (tan_h, tan),
            (load_h, load),
            (quad_h, quad),
        )
    ):
        copy = pltpu.make_async_copy(src, dst, ld.at[i])
        copy.start()
        loads.append(copy)
    c_dmg, c_disp, c_dest, c_lists, c_cols, c_lap, c_smat, c_hist, c_tan, c_load, c_quad = loads

    c_dmg.wait()
    damage = dmg[...]
    grp_d[blk] = damage.astype(BF16)
    c_disp.wait()
    root = jnp.sqrt((1.0 - damage) ** 2 + 0.001)
    grp_w[blk] = (root * disp[...]).astype(BF16)
    c_dest.wait()
    pl.semaphore_wait(barrier, g1 + g2)

    @pl.loop(1, nb)
    def _(j):
        p = dom * nb + lax.rem(blk + j, nb)
        send(grp_d.at[blk], grp_d.at[blk], ss.at[0], rs.at[0], p)

    @pl.loop(1, g1)
    def _(j):
        send(dall.at[me], dall.at[me], ss.at[1], rs.at[1], base + lax.rem(me + j, g1))

    @pl.loop(1, nb)
    def _(j):
        p = dom * nb + lax.rem(blk + j, nb)
        send(grp_w.at[blk], grp_w.at[blk], ss.at[2], rs.at[2], p)

    c_lists.wait()
    for side in range(2):
        row = lax.broadcasted_iota(jnp.int32, (nb * rows, gmax), 0)
        pickhot[side] = as_bf16(row == lists[side : side + 1, :])

    bytes_wait(dall.at[pl.ds(0, g1 - 1)], rs.at[1])

    @pl.loop(1, g2)
    def _(j):
        part = dall.at[pl.ds(base, g1)]
        send(part, part, ss.at[3], rs.at[3], lax.rem(me + g1 * j, n))

    def pick(grp, out, ghost, at):
        for side in range(2):
            total = None
            for b in range(nb):
                part = dot(grp[b], pickhot[side, b * rows : (b + 1) * rows, :])
                total = part if total is None else total + part
            out[side] = total.astype(BF16)

        @pl.when(dom > 0)
        def _():
            send(out.at[0], ghost.at[1], ss.at[at], rs.at[at + 1], me - nb)

        @pl.when(dom < nd - 1)
        def _():
            send(out.at[1], ghost.at[0], ss.at[at + 1], rs.at[at], me + nb)

    bytes_wait(grp_d.at[pl.ds(0, nb - 1)], rs.at[0])
    pick(grp_d, pick_d, ghost_d, 4)
    bytes_wait(grp_w.at[pl.ds(0, nb - 1)], rs.at[2])
    pick(grp_w, pick_w, ghost_w, 6)

    c_cols.wait()
    for k in range(kblk):
        entry = lax.broadcasted_iota(jnp.int32, (nearhot.shape[0], rows), 0)
        nearhot[:, k * rows : (k + 1) * rows] = as_bf16(entry == cols[k : k + 1, :])
    before = as_bf16(
        lax.broadcasted_iota(jnp.int32, (rows, rows), 0) < lax.broadcasted_iota(jnp.int32, (rows, rows), 1)
    )
    mine = dall[me]
    sent = lax.broadcasted_iota(jnp.int32, (n, rows), 0) == jnp.right_shift(mine, shift)
    rank = dot(as_bf16(sent), before)
    for r in range(2):
        ohm[r] = as_bf16(sent & (rank == r))
    c_smat.wait()

    @pl.loop(0, smat.shape[0])
    def _(q):
        hi, lo = halves(smat[q])
        s_hi[q] = hi
        s_lo[q] = lo

    bytes_wait(dall.at[pl.ds(0, n - g1)], rs.at[3])
    dest = dall[:, 0, :]
    wanted = jnp.right_shift(dest, shift) == me
    slot = jnp.bitwise_and(dest, rows - 1).astype(F32)
    order = dot(as_bf16(wanted), before)
    lane = lax.broadcasted_iota(jnp.int32, (n, rows), 1).astype(F32)
    own = []
    for r in range(2):
        held = jnp.sum(jnp.where(wanted & (order == r), slot + 1.0, 0.0), axis=1, keepdims=True)
        own.append(as_bf16(lane + 1.0 == held))

    def ghosts(ghost, at):
        for side, there in ((0, dom > 0), (1, dom < nd - 1)):

            @pl.when(there)
            def _():
                bytes_wait(ghost.at[side], rs.at[at + side])

            @pl.when(jnp.logical_not(there))
            def _():
                ghost[side] = jnp.zeros(ghost.shape[1:], BF16)

    def gather(grp, ghost, near):
        total = None
        for b in range(nb):
            part = dot(grp[b], nearhot[b * rows : (b + 1) * rows, :])
            total = part if total is None else total + part
        for side in range(2):
            first = nb * rows + side * gmax
            total = total + dot(ghost[side], nearhot[first : first + gmax, :])
        for k in range(kblk):
            near[k] = total[:, k * rows : (k + 1) * rows]

    ghosts(ghost_d, 4)
    gather(grp_d, ghost_d, near_d)
    c_lap.wait()
    block_rows(lap, near_d, diffuse)

    fields = jnp.concatenate([disp[...], diffuse[...], dmg[...]], axis=0)
    f_hi, f_lo = halves(fields)
    for r in range(2):
        h2s[:, 0, r * wl : r * wl + 3 * width] = dot_nt(own[r], f_hi) + dot_nt(own[r], f_lo)

    def exchange(src, dst, at):
        pltpu.make_async_copy(src.at[me], dst.at[me], rs.at[at]).start()

        @pl.loop(0, n)
        def _(j):
            p = lax.rem(me + n // 2 + j, n)

            @pl.when(j != n // 2)
            def _():
                send(src.at[p], dst.at[me], ss.at[at], rs.at[at], p)

    exchange(h2s, h2r, 8)

    ghosts(ghost_w, 6)
    gather(grp_w, ghost_w, near_w)
    c_tan.wait()
    block_rows(tan, near_w, mech)
    c_load.wait()
    damage = dmg[...]
    root = jnp.sqrt((1.0 - damage) ** 2 + 0.001)
    mech_res = root * mech[...] - load[...]
    mech[...] = mech_res
    mech_part = jnp.sum(mech_res * mech_res)

    c_hist.wait()
    c_quad.wait()
    bytes_wait(h2r, rs.at[8])
    got = None
    for r in range(2):
        g_hi, g_lo = halves(jnp.transpose(h2r[:, 0, r * wl : r * wl + 3 * width]))
        part = dot(g_hi, ohm[r]) + dot(g_lo, ohm[r])
        got = part if got is None else got + part
    u_hi, u_lo = halves(got[:width])
    u_cat = jnp.concatenate([u_hi, u_lo], axis=1)

    def points(q, source):
        st = dot(s_hi[q], u_cat) + dot(s_lo[q], u_cat)
        st = st[:, :rows] + st[:, rows:]
        return source + quad[q] * jnp.maximum(hist[q], 0.5 * st * st)

    source = lax.fori_loop(0, smat.shape[0], points, jnp.zeros((width, rows), F32), unroll=3)
    there = got[2 * width :]
    dmg_res = got[width : 2 * width] + (1.0 + 2.0 * source) * there - 2.0 * source
    dmg_part = jnp.sum(dmg_res * dmg_res)

    pad = jnp.concatenate([dmg_res, jnp.zeros((LANES - width, rows), F32)], axis=0)
    p_hi, p_lo = halves(pad)
    lane = lax.broadcasted_iota(jnp.int32, (n, LANES), 1)
    for r in range(2):
        back = dot_nt(ohm[r], p_hi) + dot_nt(ohm[r], p_lo)
        if r == 0:
            back = jnp.where(lane == width, mech_part, jnp.where(lane == width + 1, dmg_part, back))
        h3s[:, 0, r * LANES : (r + 1) * LANES] = back
    exchange(h3s, h3r, 9)

    bytes_wait(h3r, rs.at[9])
    first = h3r[:, 0, :LANES]
    total = None
    for r in range(2):
        g_hi, g_lo = halves(jnp.transpose(h3r[:, 0, r * LANES : r * LANES + width]))
        part = dot(g_hi, own[r]) + dot(g_lo, own[r])
        total = part if total is None else total + part
    entries = n * rows * width
    sums = jnp.sum(first, axis=0, keepdims=True)
    norms = jnp.sqrt(sums * (1.0 / entries) + 1e-06)
    mech_o[...] = mech[...] / norms[:, width : width + 1]
    dmg_o[...] = total / norms[:, width + 1 : width + 2]
    norm_o[...] = norms

    bytes_wait(grp_d.at[pl.ds(0, nb - 1)], ss.at[0])
    bytes_wait(dall.at[pl.ds(0, g1 - 1)], ss.at[1])
    bytes_wait(grp_w.at[pl.ds(0, nb - 1)], ss.at[2])
    bytes_wait(dall.at[pl.ds(0, n - g1)], ss.at[3])
    for at, ghost in ((4, ghost_d), (6, ghost_w)):

        @pl.when(dom > 0)
        def _():
            bytes_wait(ghost.at[0], ss.at[at])

        @pl.when(dom < nd - 1)
        def _():
            bytes_wait(ghost.at[1], ss.at[at + 1])

    bytes_wait(h2s.at[pl.ds(0, n - 1)], ss.at[8])
    bytes_wait(h3s.at[pl.ds(0, n - 1)], ss.at[9])


def on_device(
    nd,
    nb,
    displacement,
    damage,
    applied_load,
    tangent,
    laplacian,
    block_columns,
    send_lists,
    hist_mech,
    mech_dest,
    strain_matrix,
    quad_weight,
):
    n = nd * nb
    rows, width = displacement.shape
    kblk = block_columns.shape[1]
    points = hist_mech.shape[1]
    gmax = send_lists.shape[2]
    wl = -(-3 * width // LANES) * LANES
    args = (
        displacement.T,
        damage.T,
        applied_load.T,
        jnp.transpose(tangent, (1, 2, 3, 0)),
        jnp.transpose(laplacian, (1, 2, 3, 0)),
        block_columns.T,
        send_lists[0],
        jnp.transpose(hist_mech, (1, 2, 0)),
        mech_dest.reshape(1, rows),
        strain_matrix,
        quad_weight,
    )
    vmem = pltpu.VMEM
    mech_out, dmg_out, norms = pl.pallas_call(
        functools.partial(kernel, nd, nb),
        out_shape=(
            jax.ShapeDtypeStruct((width, rows), F32),
            jax.ShapeDtypeStruct((width, rows), F32),
            jax.ShapeDtypeStruct((1, LANES), F32),
        ),
        in_specs=[pl.BlockSpec(memory_space=pl.ANY)] * len(args),
        out_specs=[pl.BlockSpec(memory_space=vmem)] * 3,
        scratch_shapes=[
            vmem((width, rows), F32),
            vmem((width, rows), F32),
            vmem((width, rows), F32),
            vmem((kblk, width, width, rows), BF16),
            vmem((kblk, width, width, rows), BF16),
            vmem((kblk, rows), jnp.int32),
            vmem((2, gmax), jnp.int32),
            vmem((points, width, rows), F32),
            vmem((points, width, width), F32),
            pltpu.SMEM((points,), F32),
            vmem((n, 1, rows), jnp.int32),
            vmem((nb, width, rows), BF16),
            vmem((nb, width, rows), BF16),
            vmem((2, width, gmax), BF16),
            vmem((2, width, gmax), BF16),
            vmem((2, width, gmax), BF16),
            vmem((2, width, gmax), BF16),
            vmem((2, nb * rows, gmax), BF16),
            vmem((nb * rows + 2 * gmax, kblk * rows), BF16),
            vmem((kblk, width, rows), F32),
            vmem((kblk, width, rows), F32),
            vmem((points, width, width), BF16),
            vmem((points, width, width), BF16),
            vmem((width, rows), F32),
            vmem((width, rows), F32),
            vmem((2, n, rows), BF16),
            vmem((n, 1, 2 * wl), F32),
            vmem((n, 1, 2 * wl), F32),
            vmem((n, 1, 2 * LANES), F32),
            vmem((n, 1, 2 * LANES), F32),
            pltpu.SemaphoreType.DMA((11,)),
            pltpu.SemaphoreType.DMA((10,)),
            pltpu.SemaphoreType.DMA((10,)),
        ],
        compiler_params=pltpu.CompilerParams(
            collective_id=0, has_side_effects=True, vmem_limit_bytes=60 << 20
        ),
        name="fracture_pass",
    )(*args)
    return mech_out.T, dmg_out.T, norms[0, width : width + 2]


def solution(mesh):
    both = ("dom", "blk")
    in_specs = (
        P(both, None),
        P(both, None),
        P(both, None),
        P(both, None, None, None),
        P(both, None, None, None),
        P(both, None),
        P("dom", None, None),
        P(both, None, None),
        P(both),
        P(),
        P(),
    )
    return jax.shard_map(
        functools.partial(on_device, mesh.shape["dom"], mesh.shape["blk"]),
        mesh=mesh,
        in_specs=in_specs,
        out_specs=(P(both, None), P(both, None), P()),
        check_vma=False,
    )
```

```python
import functools
import math

import jax
import jax.numpy as jnp
from jax import lax
from jax.experimental import pallas as pl
from jax.experimental.pallas import tpu as pltpu
from jax.sharding import PartitionSpec as P

MESH = pl.DeviceIdType.MESH
F32 = jnp.float32
BF16 = jnp.bfloat16
LANES = 128


def dot(a, b):
    return jnp.dot(a, b, preferred_element_type=F32)


def dot_nt(a, b):
    return lax.dot_general(a, b, (((1,), (1,)), ((), ())), preferred_element_type=F32)


def halves(x):
    hi = x.astype(BF16)
    return hi, (x - hi.astype(F32)).astype(BF16)


def as_bf16(mask):
    return jnp.where(mask, 1.0, 0.0).astype(BF16)


def bytes_wait(ref, sem):
    pltpu.make_async_copy(ref, ref, sem).wait()


def block_rows(mat, near, out):
    kblk, width = near.shape[0], near.shape[1]

    def rows(rb, carry):
        r0 = pl.multiple_of(rb * 8, 8)
        acc = None
        for k in range(kblk):
            for c in range(0, width, 16):
                part = mat[k, pl.ds(r0, 8), c : c + 16, :].astype(F32) * near[k, c : c + 16, :][None]
                acc = part if acc is None else acc + part
        out[pl.ds(r0, 8), :] = jnp.sum(acc, axis=1)
        return carry

    lax.fori_loop(0, width // 8, rows, 0)


def kernel(
    nd,
    nb,
    disp_h,
    dmg_h,
    load_h,
    tan_h,
    lap_h,
    cols_h,
    lists_h,
    hist_h,
    dest_h,
    smat_h,
    quad_h,
    mech_o,
    dmg_o,
    norm_o,
    disp,
    dmg,
    load,
    tan,
    lap,
    cols,
    lists,
    hist,
    smat,
    quad,
    dall,
    grp_d,
    grp_w,
    pick_d,
    pick_w,
    ghost_d,
    ghost_w,
    pickhot,
    nearhot,
    near_d,
    near_w,
    s_hi,
    s_lo,
    diffuse,
    mech,
    ohm,
    h2s,
    h2r,
    h3s,
    h3r,
    ld,
    ss,
    rs,
):
    n = nd * nb
    g1 = 2 * nb
    g2 = n // g1
    width, rows = disp.shape
    kblk = cols.shape[0]
    gmax = lists.shape[1]
    shift = rows.bit_length() - 1
    dom = lax.axis_index("dom")
    blk = lax.axis_index("blk")
    me = dom * nb + blk
    base = (me // g1) * g1

    side = math.isqrt(g2)

    def hops(up):
        z, x = divmod(up, side)
        return min(z, side - z) + min(x, side - x)

    far_groups = sorted(range(g2), key=hops, reverse=True)
    far_peers = range(g1 - 1, -1, -1)

    def loc(p):
        return (p // nb, lax.rem(p, nb))

    def signal(p):
        pl.semaphore_signal(barrier, inc=1, device_id=loc(p), device_id_type=MESH)

    def send(src, dst, s, r, p):
        pltpu.make_async_remote_copy(
            src_ref=src, dst_ref=dst, send_sem=s, recv_sem=r, device_id=loc(p), device_id_type=MESH
        ).start()

    barrier = pltpu.get_barrier_semaphore()

    @pl.loop(1, g1)
    def _(j):
        signal(base + lax.rem(me + j, g1))

    @pl.loop(1, g2)
    def _(j):
        signal(lax.rem(me + g1 * j, n))

    signal(lax.rem(me + nb, n))
    signal(lax.rem(me + n - nb, n))

    loads = []
    for i, (src, dst) in enumerate(
        (
            (dmg_h, dmg),
            (disp_h, disp),
            (dest_h, dall.at[me]),
            (lists_h, lists),
            (cols_h, cols),
            (lap_h, lap),
            (smat_h, smat),
            (hist_h, hist),
            (tan_h, tan),
            (load_h, load),
            (quad_h, quad),
        )
    ):
        copy = pltpu.make_async_copy(src, dst, ld.at[i])
        copy.start()
        loads.append(copy)
    c_dmg, c_disp, c_dest, c_lists, c_cols, c_lap, c_smat, c_hist, c_tan, c_load, c_quad = loads

    c_dmg.wait()
    damage = dmg[...]
    grp_d[blk] = damage.astype(BF16)
    c_disp.wait()
    root = jnp.sqrt((1.0 - damage) ** 2 + 0.001)
    grp_w[blk] = (root * disp[...]).astype(BF16)
    c_dest.wait()
    pl.semaphore_wait(barrier, g1 + g2)

    @pl.loop(1, g1)
    def _(j):
        send(dall.at[me], dall.at[me], ss.at[1], rs.at[1], base + lax.rem(me + j, g1))

    @pl.loop(1, nb)
    def _(j):
        p = dom * nb + lax.rem(blk + j, nb)
        send(grp_d.at[blk], grp_d.at[blk], ss.at[0], rs.at[0], p)

    @pl.loop(1, nb)
    def _(j):
        p = dom * nb + lax.rem(blk + j, nb)
        send(grp_w.at[blk], grp_w.at[blk], ss.at[2], rs.at[2], p)

    c_lists.wait()
    for side in range(2):
        row = lax.broadcasted_iota(jnp.int32, (nb * rows, gmax), 0)
        pickhot[side] = as_bf16(row == lists[side : side + 1, :])

    bytes_wait(dall.at[pl.ds(0, g1 - 1)], rs.at[1])

    @pl.loop(1, g2)
    def _(j):
        part = dall.at[pl.ds(base, g1)]
        send(part, part, ss.at[3], rs.at[3], lax.rem(me + g1 * j, n))

    def pick(grp, out, ghost, at):
        for side in range(2):
            total = None
            for b in range(nb):
                part = dot(grp[b], pickhot[side, b * rows : (b + 1) * rows, :])
                total = part if total is None else total + part
            out[side] = total.astype(BF16)

        @pl.when(dom > 0)
        def _():
            send(out.at[0], ghost.at[1], ss.at[at], rs.at[at + 1], me - nb)

        @pl.when(dom < nd - 1)
        def _():
            send(out.at[1], ghost.at[0], ss.at[at + 1], rs.at[at], me + nb)

    bytes_wait(grp_d.at[pl.ds(0, nb - 1)], rs.at[0])
    pick(grp_d, pick_d, ghost_d, 4)
    bytes_wait(grp_w.at[pl.ds(0, nb - 1)], rs.at[2])
    pick(grp_w, pick_w, ghost_w, 6)

    c_cols.wait()
    for k in range(kblk):
        entry = lax.broadcasted_iota(jnp.int32, (nearhot.shape[0], rows), 0)
        nearhot[:, k * rows : (k + 1) * rows] = as_bf16(entry == cols[k : k + 1, :])
    before = as_bf16(
        lax.broadcasted_iota(jnp.int32, (rows, rows), 0) < lax.broadcasted_iota(jnp.int32, (rows, rows), 1)
    )
    mine = dall[me]
    sent = lax.broadcasted_iota(jnp.int32, (n, rows), 0) == jnp.right_shift(mine, shift)
    rank = dot(as_bf16(sent), before)
    for r in range(2):
        ohm[r] = as_bf16(sent & (rank == r))
    c_smat.wait()

    @pl.loop(0, smat.shape[0])
    def _(q):
        hi, lo = halves(smat[q])
        s_hi[q] = hi
        s_lo[q] = lo

    def ghosts(ghost, at):
        for side, there in ((0, dom > 0), (1, dom < nd - 1)):

            @pl.when(there)
            def _():
                bytes_wait(ghost.at[side], rs.at[at + side])

            @pl.when(jnp.logical_not(there))
            def _():
                ghost[side] = jnp.zeros(ghost.shape[1:], BF16)

    def gather(grp, ghost, near):
        total = None
        for b in range(nb):
            part = dot(grp[b], nearhot[b * rows : (b + 1) * rows, :])
            total = part if total is None else total + part
        for side in range(2):
            first = nb * rows + side * gmax
            total = total + dot(ghost[side], nearhot[first : first + gmax, :])
        for k in range(kblk):
            near[k] = total[:, k * rows : (k + 1) * rows]

    ghosts(ghost_d, 4)
    gather(grp_d, ghost_d, near_d)
    c_lap.wait()
    block_rows(lap, near_d, diffuse)

    bytes_wait(dall.at[pl.ds(0, n - g1)], rs.at[3])
    dest = dall[:, 0, :]
    wanted = jnp.right_shift(dest, shift) == me
    slot = jnp.bitwise_and(dest, rows - 1).astype(F32)
    order = dot(as_bf16(wanted), before)
    lane = lax.broadcasted_iota(jnp.int32, (n, rows), 1).astype(F32)
    own = []
    for r in range(2):
        held = jnp.sum(jnp.where(wanted & (order == r), slot + 1.0, 0.0), axis=1, keepdims=True)
        own.append(as_bf16(lane + 1.0 == held))

    fields = jnp.concatenate([disp[...], diffuse[...], dmg[...]], axis=0)
    f_hi, f_lo = halves(fields)
    both = jnp.concatenate(own, axis=1)
    void = jnp.zeros(f_hi.shape, BF16)

    def twice(f):
        top = jnp.concatenate([f, void], axis=1)
        low = jnp.concatenate([void, f], axis=1)
        return jnp.concatenate([top, low], axis=0)

    h2s[:, 0, : 6 * width] = dot_nt(both, twice(f_hi)) + dot_nt(both, twice(f_lo))

    def exchange(src, dst, at):
        pltpu.make_async_copy(src.at[me], dst.at[me], rs.at[at]).start()

        for up in far_groups:
            first = lax.rem(base + up * g1, n)
            for low in far_peers:
                if up or low:
                    p = first + jnp.bitwise_xor(me - base, low)
                    send(src.at[p], dst.at[me], ss.at[at], rs.at[at], p)

    exchange(h2s, h2r, 8)

    ghosts(ghost_w, 6)
    gather(grp_w, ghost_w, near_w)
    c_tan.wait()
    block_rows(tan, near_w, mech)
    c_load.wait()
    damage = dmg[...]
    root = jnp.sqrt((1.0 - damage) ** 2 + 0.001)
    mech_res = root * mech[...] - load[...]
    mech[...] = mech_res
    mech_part = jnp.sum(mech_res * mech_res)

    c_hist.wait()
    c_quad.wait()
    bytes_wait(h2r, rs.at[8])
    g_hi, g_lo = halves(jnp.transpose(h2r[:, 0, : 6 * width]))
    got = None
    for r in range(2):
        rows_r = slice(r * 3 * width, (r + 1) * 3 * width)
        part = dot(g_hi[rows_r], ohm[r]) + dot(g_lo[rows_r], ohm[r])
        got = part if got is None else got + part
    u_hi, u_lo = halves(got[:width])
    u_cat = jnp.concatenate([u_hi, u_lo], axis=1)

    def points(q, source):
        st = dot(s_hi[q], u_cat) + dot(s_lo[q], u_cat)
        st = st[:, :rows] + st[:, rows:]
        return source + quad[q] * jnp.maximum(hist[q], 0.5 * st * st)

    source = lax.fori_loop(0, smat.shape[0], points, jnp.zeros((width, rows), F32), unroll=True)
    there = got[2 * width :]
    dmg_res = got[width : 2 * width] + (1.0 + 2.0 * source) * there - 2.0 * source
    dmg_part = jnp.sum(dmg_res * dmg_res)

    pad = jnp.concatenate([dmg_res, jnp.zeros((LANES - width, rows), F32)], axis=0)
    p_hi, p_lo = halves(pad)
    lane = lax.broadcasted_iota(jnp.int32, (n, LANES), 1)
    for r in range(2):
        back = dot_nt(ohm[r], p_hi) + dot_nt(ohm[r], p_lo)
        if r == 0:
            back = jnp.where(lane == width, mech_part, jnp.where(lane == width + 1, dmg_part, back))
        h3s[:, 0, r * LANES : (r + 1) * LANES] = back
    exchange(h3s, h3r, 9)

    bytes_wait(h3r, rs.at[9])
    first = h3r[:, 0, :LANES]
    total = None
    for r in range(2):
        g_hi, g_lo = halves(jnp.transpose(h3r[:, 0, r * LANES : r * LANES + width]))
        part = dot(g_hi, own[r]) + dot(g_lo, own[r])
        total = part if total is None else total + part
    entries = n * rows * width
    sums = jnp.sum(first, axis=0, keepdims=True)
    norms = jnp.sqrt(sums * (1.0 / entries) + 1e-06)
    mech_o[...] = mech[...]
    dmg_o[...] = total
    norm_o[...] = norms[:, width : width + 2]

    bytes_wait(grp_d.at[pl.ds(0, nb - 1)], ss.at[0])
    bytes_wait(dall.at[pl.ds(0, g1 - 1)], ss.at[1])
    bytes_wait(grp_w.at[pl.ds(0, nb - 1)], ss.at[2])
    bytes_wait(dall.at[pl.ds(0, n - g1)], ss.at[3])
    for at, ghost in ((4, ghost_d), (6, ghost_w)):

        @pl.when(dom > 0)
        def _():
            bytes_wait(ghost.at[0], ss.at[at])

        @pl.when(dom < nd - 1)
        def _():
            bytes_wait(ghost.at[1], ss.at[at + 1])

    bytes_wait(h2s.at[pl.ds(0, n - 1)], ss.at[8])
    bytes_wait(h3s.at[pl.ds(0, n - 1)], ss.at[9])


def normalize(mech, dmg, norm, mech_o, dmg_o, norm_o):
    norms = norm[...]
    mech_o[...] = mech[...] / norms[:, 0:1]
    dmg_o[...] = dmg[...] / norms[:, 1:2]
    norm_o[...] = norms


def on_device(
    nd,
    nb,
    displacement,
    damage,
    applied_load,
    tangent,
    laplacian,
    block_columns,
    send_lists,
    hist_mech,
    mech_dest,
    strain_matrix,
    quad_weight,
):
    n = nd * nb
    rows, width = displacement.shape
    kblk = block_columns.shape[1]
    points = hist_mech.shape[1]
    gmax = send_lists.shape[2]
    wl = -(-6 * width // LANES) * LANES
    args = (
        displacement.T,
        damage.T,
        applied_load.T,
        jnp.transpose(tangent, (1, 2, 3, 0)),
        jnp.transpose(laplacian, (1, 2, 3, 0)),
        block_columns.T,
        send_lists[0],
        jnp.transpose(hist_mech, (1, 2, 0)),
        mech_dest.reshape(1, rows),
        strain_matrix,
        quad_weight,
    )
    vmem = pltpu.VMEM
    residuals = pl.pallas_call(
        functools.partial(kernel, nd, nb),
        out_shape=(
            jax.ShapeDtypeStruct((width, rows), F32),
            jax.ShapeDtypeStruct((width, rows), F32),
            jax.ShapeDtypeStruct((1, 2), F32),
        ),
        in_specs=[pl.BlockSpec(memory_space=pl.ANY)] * len(args),
        out_specs=[pl.BlockSpec(memory_space=vmem)] * 3,
        scratch_shapes=[
            vmem((width, rows), F32),
            vmem((width, rows), F32),
            vmem((width, rows), F32),
            vmem((kblk, width, width, rows), BF16),
            vmem((kblk, width, width, rows), BF16),
            vmem((kblk, rows), jnp.int32),
            vmem((2, gmax), jnp.int32),
            vmem((points, width, rows), F32),
            vmem((points, width, width), F32),
            pltpu.SMEM((points,), F32),
            vmem((n, 1, rows), jnp.int32),
            vmem((nb, width, rows), BF16),
            vmem((nb, width, rows), BF16),
            vmem((2, width, gmax), BF16),
            vmem((2, width, gmax), BF16),
            vmem((2, width, gmax), BF16),
            vmem((2, width, gmax), BF16),
            vmem((2, nb * rows, gmax), BF16),
            vmem((nb * rows + 2 * gmax, kblk * rows), BF16),
            vmem((kblk, width, rows), F32),
            vmem((kblk, width, rows), F32),
            vmem((points, width, width), BF16),
            vmem((points, width, width), BF16),
            vmem((width, rows), F32),
            vmem((width, rows), F32),
            vmem((2, n, rows), BF16),
            vmem((n, 1, wl), F32),
            vmem((n, 1, wl), F32),
            vmem((n, 1, 2 * LANES), F32),
            vmem((n, 1, 2 * LANES), F32),
            pltpu.SemaphoreType.DMA((11,)),
            pltpu.SemaphoreType.DMA((10,)),
            pltpu.SemaphoreType.DMA((10,)),
        ],
        compiler_params=pltpu.CompilerParams(
            collective_id=0, has_side_effects=True, vmem_limit_bytes=60 << 20
        ),
        name="fracture_pass",
    )(*args)
    mech_out, dmg_out, norms = pl.pallas_call(
        normalize,
        out_shape=(
            jax.ShapeDtypeStruct((width, rows), F32),
            jax.ShapeDtypeStruct((width, rows), F32),
            jax.ShapeDtypeStruct((1, 2), F32),
        ),
        name="normalize",
    )(*residuals)
    return mech_out.T, dmg_out.T, norms.reshape(2)


def solution(mesh):
    both = ("dom", "blk")
    in_specs = (
        P(both, None),
        P(both, None),
        P(both, None),
        P(both, None, None, None),
        P(both, None, None, None),
        P(both, None),
        P("dom", None, None),
        P(both, None, None),
        P(both),
        P(),
        P(),
    )
    return jax.shard_map(
        functools.partial(on_device, mesh.shape["dom"], mesh.shape["blk"]),
        mesh=mesh,
        in_specs=in_specs,
        out_specs=(P(both, None), P(both, None), P()),
        check_vma=False,
    )
```

```python
import functools
import math

import jax
import jax.numpy as jnp
from jax import lax
from jax.experimental import pallas as pl
from jax.experimental.pallas import tpu as pltpu
from jax.sharding import PartitionSpec as P

MESH = pl.DeviceIdType.MESH
F32 = jnp.float32
BF16 = jnp.bfloat16
LANES = 128


def dot(a, b):
    return jnp.dot(a, b, preferred_element_type=F32)


def dot_nt(a, b):
    return lax.dot_general(a, b, (((1,), (1,)), ((), ())), preferred_element_type=F32)


def halves(x):
    hi = x.astype(BF16)
    return hi, (x - hi.astype(F32)).astype(BF16)


def as_bf16(mask):
    return jnp.where(mask, 1.0, 0.0).astype(BF16)


def bytes_wait(ref, sem):
    pltpu.make_async_copy(ref, ref, sem).wait()


def block_rows(mat, near, out):
    kblk, width = near.shape[0], near.shape[1]

    def rows(rb, carry):
        r0 = pl.multiple_of(rb * 8, 8)
        acc = None
        for k in range(kblk):
            for c in range(0, width, 16):
                part = mat[k, pl.ds(r0, 8), c : c + 16, :].astype(F32) * near[k, c : c + 16, :][None]
                acc = part if acc is None else acc + part
        out[pl.ds(r0, 8), :] = jnp.sum(acc, axis=1)
        return carry

    lax.fori_loop(0, width // 8, rows, 0)


def kernel(
    nd,
    nb,
    disp_h,
    dmg_h,
    load_h,
    tan_h,
    lap_h,
    cols_h,
    lists_h,
    hist_h,
    dest_h,
    smat_h,
    quad_h,
    mech_o,
    dmg_o,
    norm_o,
    disp,
    dmg,
    load,
    tan,
    lap,
    cols,
    lists,
    hist,
    smat,
    quad,
    dall,
    grp_d,
    grp_w,
    pick_d,
    pick_w,
    ghost_d,
    ghost_w,
    pickhot,
    nearhot,
    near_d,
    near_w,
    s_cat,
    diffuse,
    mech,
    ohm,
    h2s,
    h2r,
    h3s,
    h3r,
    ld,
    ss,
    rs,
):
    n = nd * nb
    g1 = 2 * nb
    side = math.isqrt(n // g1)
    width, rows = disp.shape
    kblk = cols.shape[0]
    gmax = lists.shape[1]
    shift = rows.bit_length() - 1
    dom = lax.axis_index("dom")
    blk = lax.axis_index("blk")
    core = lax.rem(dom, 2)
    z, x = dom // (2 * side), lax.rem(dom // 2, side)
    me = dom * nb + blk
    cy = core * nb + blk

    def at(z, x, cy):
        return (z * side + x) * g1 + cy

    def turn(c, step):
        return lax.rem(c + step, side)

    def hops(zx):
        return sum(min(c, side - c) for c in zx)

    far_groups = sorted(((a, b) for a in range(side) for b in range(side)), key=hops, reverse=True)
    far_peers = range(g1 - 1, -1, -1)
    peers_x = [at(z, turn(x, step), cy) for step in range(1, side)]
    peers_z = [at(turn(z, step), x, cy) for step in range(1, side)]
    peers_cy = [at(z, x, jnp.bitwise_xor(cy, step)) for step in range(1, g1)]
    peers_y = [at(z, x, core * nb + lax.rem(blk + step, nb)) for step in range(1, nb)]
    across = lax.rem(jnp.where(core == 0, dom + nd - 1, dom + 1), nd) * nb + blk

    def loc(p):
        return (p // nb, lax.rem(p, nb))

    def send(src, dst, s, r, p):
        pltpu.make_async_remote_copy(
            src_ref=src, dst_ref=dst, send_sem=s, recv_sem=r, device_id=loc(p), device_id_type=MESH
        ).start()

    barrier = pltpu.get_barrier_semaphore()
    greeted = [across, *peers_x, *peers_z, *peers_cy]
    for p in greeted:
        pl.semaphore_signal(barrier, inc=1, device_id=loc(p), device_id_type=MESH)

    loads = []
    for i, (src, dst) in enumerate(
        (
            (dest_h, dall.at[z, x, cy]),
            (dmg_h, dmg),
            (disp_h, disp),
            (lists_h, lists),
            (cols_h, cols),
            (lap_h, lap),
            (smat_h, smat),
            (hist_h, hist),
            (tan_h, tan),
            (load_h, load),
            (quad_h, quad),
        )
    ):
        copy = pltpu.make_async_copy(src, dst, ld.at[i])
        copy.start()
        loads.append(copy)
    c_dest, c_dmg, c_disp, c_lists, c_cols, c_lap, c_smat, c_hist, c_tan, c_load, c_quad = loads

    c_dmg.wait()
    damage = dmg[...]
    grp_d[blk] = damage.astype(BF16)
    c_dest.wait()
    pl.semaphore_wait(barrier, len(greeted))

    def spread(part, peers, i):
        for p in peers:
            send(part, part, ss.at[i], rs.at[i], p)

    spread(dall.at[z, x, cy], peers_x, 0)
    spread(grp_d.at[blk], peers_y, 1)

    c_disp.wait()
    root = jnp.sqrt((1.0 - damage) ** 2 + 0.001)
    grp_w[blk] = (root * disp[...]).astype(BF16)
    spread(grp_w.at[blk], peers_y, 3)
    c_lists.wait()
    for which in range(2):
        row = lax.broadcasted_iota(jnp.int32, (nb * rows, gmax), 0)
        pickhot[which] = as_bf16(row == lists[which : which + 1, :])

    bytes_wait(dall.at[0, pl.ds(0, side - 1), 0], rs.at[0])
    spread(dall.at[z, :, cy], peers_z, 2)

    def pick(grp, out, ghost, i):
        for which in range(2):
            total = None
            for b in range(nb):
                part = dot(grp[b], pickhot[which, b * rows : (b + 1) * rows, :])
                total = part if total is None else total + part
            out[which] = total.astype(BF16)

        @pl.when(dom > 0)
        def _():
            send(out.at[0], ghost.at[1], ss.at[i], rs.at[i + 1], me - nb)

        @pl.when(dom < nd - 1)
        def _():
            send(out.at[1], ghost.at[0], ss.at[i + 1], rs.at[i], me + nb)

    bytes_wait(grp_d.at[pl.ds(0, nb - 1)], rs.at[1])
    pick(grp_d, pick_d, ghost_d, 4)

    c_cols.wait()
    for k in range(kblk):
        entry = lax.broadcasted_iota(jnp.int32, (nearhot.shape[0], rows), 0)
        nearhot[:, k * rows : (k + 1) * rows] = as_bf16(entry == cols[k : k + 1, :])
    before = as_bf16(
        lax.broadcasted_iota(jnp.int32, (rows, rows), 0) < lax.broadcasted_iota(jnp.int32, (rows, rows), 1)
    )
    mine = dall[z, x, cy]
    sent = lax.broadcasted_iota(jnp.int32, (n, rows), 0) == jnp.right_shift(mine, shift)
    rank = dot(as_bf16(sent), before)
    for r in range(2):
        ohm[r] = as_bf16(sent & (rank == r))

    bytes_wait(grp_w.at[pl.ds(0, nb - 1)], rs.at[3])
    pick(grp_w, pick_w, ghost_w, 6)

    bytes_wait(dall.at[pl.ds(0, side - 1), :, 0], rs.at[2])
    spread(dall.at[:, :, cy], peers_cy, 8)

    def ghosts(ghost, i):
        for which, there in ((0, dom > 0), (1, dom < nd - 1)):

            @pl.when(there)
            def _():
                bytes_wait(ghost.at[which], rs.at[i + which])

            @pl.when(jnp.logical_not(there))
            def _():
                ghost[which] = jnp.zeros(ghost.shape[1:], BF16)

    def gather(grp, ghost, near):
        total = None
        for b in range(nb):
            part = dot(grp[b], nearhot[b * rows : (b + 1) * rows, :])
            total = part if total is None else total + part
        for which in range(2):
            first = nb * rows + which * gmax
            total = total + dot(ghost[which], nearhot[first : first + gmax, :])
        for k in range(kblk):
            near[k] = total[:, k * rows : (k + 1) * rows]

    ghosts(ghost_d, 4)
    gather(grp_d, ghost_d, near_d)
    c_lap.wait()
    block_rows(lap, near_d, diffuse)

    bytes_wait(dall.at[:, :, pl.ds(0, g1 - 1)], rs.at[8])
    dest = dall[:, :, :, 0, :].reshape(n, rows)
    wanted = jnp.right_shift(dest, shift) == me
    slot = jnp.bitwise_and(dest, rows - 1).astype(F32)
    order = dot(as_bf16(wanted), before)
    lane = lax.broadcasted_iota(jnp.int32, (n, rows), 1).astype(F32)
    own = []
    for r in range(2):
        held = jnp.sum(jnp.where(wanted & (order == r), slot + 1.0, 0.0), axis=1, keepdims=True)
        own.append(as_bf16(lane + 1.0 == held))

    fields = jnp.concatenate([disp[...], diffuse[...], dmg[...]], axis=0)
    f_hi, f_lo = halves(fields)
    both = jnp.concatenate(own, axis=1)
    void = jnp.zeros(f_hi.shape, BF16)

    def twice(f):
        top = jnp.concatenate([f, void], axis=1)
        low = jnp.concatenate([void, f], axis=1)
        return jnp.concatenate([top, low], axis=0)

    h2s[:, 0, : 6 * width] = dot_nt(both, twice(f_hi)) + dot_nt(both, twice(f_lo))

    def exchange(src, dst, i):
        pltpu.make_async_copy(src.at[me], dst.at[me], rs.at[i]).start()
        for group in far_groups:
            first = at(turn(z, group[0]), turn(x, group[1]), 0)
            for low in far_peers:
                if any(group) or low:
                    p = first + jnp.bitwise_xor(cy, low)
                    send(src.at[p], dst.at[me], ss.at[i], rs.at[i], p)

    exchange(h2s, h2r, 9)

    ghosts(ghost_w, 6)
    gather(grp_w, ghost_w, near_w)
    c_tan.wait()
    block_rows(tan, near_w, mech)
    c_load.wait()
    damage = dmg[...]
    root = jnp.sqrt((1.0 - damage) ** 2 + 0.001)
    mech_res = root * mech[...] - load[...]
    mech[...] = mech_res
    mech_part = jnp.sum(mech_res * mech_res)

    c_hist.wait()
    c_quad.wait()
    c_smat.wait()

    @pl.loop(0, smat.shape[0])
    def _(q):
        hi, lo = halves(smat[q])
        gap = jnp.zeros((width, LANES - width), BF16)
        s_cat[q] = jnp.concatenate([hi, gap, lo, gap], axis=1)

    bytes_wait(h2r, rs.at[9])
    g_hi, g_lo = halves(jnp.transpose(h2r[:, 0, : 6 * width]))
    got = None
    for r in range(2):
        rows_r = slice(r * 3 * width, (r + 1) * 3 * width)
        part = dot(g_hi[rows_r], ohm[r]) + dot(g_lo[rows_r], ohm[r])
        got = part if got is None else got + part
    u_hi, u_lo = halves(got[:width])
    u_cat = jnp.concatenate([u_hi, u_lo], axis=1)
    gap = jnp.zeros((LANES - width, 2 * rows), BF16)
    u_cat = jnp.concatenate([u_cat, gap, u_cat, gap], axis=0)

    def points(q, source):
        st = dot(s_cat[q], u_cat)
        st = st[:, :rows] + st[:, rows:]
        return source + quad[q] * jnp.maximum(hist[q], 0.5 * st * st)

    source = lax.fori_loop(0, smat.shape[0], points, jnp.zeros((width, rows), F32), unroll=True)
    there = got[2 * width :]
    dmg_res = got[width : 2 * width] + (1.0 + 2.0 * source) * there - 2.0 * source
    dmg_part = jnp.sum(dmg_res * dmg_res)

    pad = jnp.concatenate([dmg_res, jnp.zeros((LANES - width, rows), F32)], axis=0)
    p_hi, p_lo = halves(pad)
    lane = lax.broadcasted_iota(jnp.int32, (n, LANES), 1)
    for r in range(2):
        back = dot_nt(ohm[r], p_hi) + dot_nt(ohm[r], p_lo)
        if r == 0:
            back = jnp.where(lane == width, mech_part, jnp.where(lane == width + 1, dmg_part, back))
        h3s[:, 0, r * LANES : (r + 1) * LANES] = back
    exchange(h3s, h3r, 10)

    bytes_wait(h3r, rs.at[10])
    first = h3r[:, 0, :LANES]
    total = None
    for r in range(2):
        g_hi, g_lo = halves(jnp.transpose(h3r[:, 0, r * LANES : r * LANES + width]))
        part = dot(g_hi, own[r]) + dot(g_lo, own[r])
        total = part if total is None else total + part
    entries = n * rows * width
    sums = jnp.sum(first, axis=0, keepdims=True)
    norms = jnp.sqrt(sums * (1.0 / entries) + 1e-06)
    mech_o[...] = mech[...]
    dmg_o[...] = total
    norm_o[...] = norms[:, width : width + 2]

    bytes_wait(dall.at[0, pl.ds(0, side - 1), 0], ss.at[0])
    bytes_wait(grp_d.at[pl.ds(0, nb - 1)], ss.at[1])
    bytes_wait(dall.at[pl.ds(0, side - 1), :, 0], ss.at[2])
    bytes_wait(grp_w.at[pl.ds(0, nb - 1)], ss.at[3])
    for i, ghost in ((4, ghost_d), (6, ghost_w)):

        @pl.when(dom > 0)
        def _():
            bytes_wait(ghost.at[0], ss.at[i])

        @pl.when(dom < nd - 1)
        def _():
            bytes_wait(ghost.at[1], ss.at[i + 1])

    bytes_wait(dall.at[:, :, pl.ds(0, g1 - 1)], ss.at[8])
    bytes_wait(h2s.at[pl.ds(0, n - 1)], ss.at[9])
    bytes_wait(h3s.at[pl.ds(0, n - 1)], ss.at[10])


def normalize(mech, dmg, norm, mech_o, dmg_o, norm_o):
    norms = norm[...]
    mech_o[...] = mech[...] / norms[:, 0:1]
    dmg_o[...] = dmg[...] / norms[:, 1:2]
    norm_o[...] = norms


def on_device(
    nd,
    nb,
    displacement,
    damage,
    applied_load,
    tangent,
    laplacian,
    block_columns,
    send_lists,
    hist_mech,
    mech_dest,
    strain_matrix,
    quad_weight,
):
    n = nd * nb
    rows, width = displacement.shape
    kblk = block_columns.shape[1]
    points = hist_mech.shape[1]
    gmax = send_lists.shape[2]
    wl = -(-6 * width // LANES) * LANES
    side = math.isqrt(nd // 2)
    args = (
        displacement.T,
        damage.T,
        applied_load.T,
        jnp.transpose(tangent, (1, 2, 3, 0)),
        jnp.transpose(laplacian, (1, 2, 3, 0)),
        block_columns.T,
        send_lists[0],
        jnp.transpose(hist_mech, (1, 2, 0)),
        mech_dest.reshape(1, rows),
        strain_matrix,
        quad_weight,
    )
    vmem = pltpu.VMEM
    residuals = pl.pallas_call(
        functools.partial(kernel, nd, nb),
        out_shape=(vmem((width, rows), F32), vmem((width, rows), F32), vmem((1, 2), F32)),
        in_specs=[pl.BlockSpec(memory_space=pl.ANY)] * len(args),
        out_specs=[pl.BlockSpec(memory_space=vmem)] * 3,
        scratch_shapes=[
            vmem((width, rows), F32),
            vmem((width, rows), F32),
            vmem((width, rows), F32),
            vmem((kblk, width, width, rows), BF16),
            vmem((kblk, width, width, rows), BF16),
            vmem((kblk, rows), jnp.int32),
            vmem((2, gmax), jnp.int32),
            vmem((points, width, rows), F32),
            vmem((points, width, width), F32),
            pltpu.SMEM((points,), F32),
            vmem((side, side, 2 * nb, 1, rows), jnp.int32),
            vmem((nb, width, rows), BF16),
            vmem((nb, width, rows), BF16),
            vmem((2, width, gmax), BF16),
            vmem((2, width, gmax), BF16),
            vmem((2, width, gmax), BF16),
            vmem((2, width, gmax), BF16),
            vmem((2, nb * rows, gmax), BF16),
            vmem((nb * rows + 2 * gmax, kblk * rows), BF16),
            vmem((kblk, width, rows), F32),
            vmem((kblk, width, rows), F32),
            vmem((points, width, 2 * LANES), BF16),
            vmem((width, rows), F32),
            vmem((width, rows), F32),
            vmem((2, n, rows), BF16),
            vmem((n, 1, wl), F32),
            vmem((n, 1, wl), F32),
            vmem((n, 1, 2 * LANES), F32),
            vmem((n, 1, 2 * LANES), F32),
            pltpu.SemaphoreType.DMA((11,)),
            pltpu.SemaphoreType.DMA((11,)),
            pltpu.SemaphoreType.DMA((11,)),
        ],
        compiler_params=pltpu.CompilerParams(
            collective_id=0, has_side_effects=True, vmem_limit_bytes=60 << 20
        ),
        name="fracture_pass",
    )(*args)
    mech_out, dmg_out, norms = pl.pallas_call(
        normalize,
        out_shape=(
            jax.ShapeDtypeStruct((width, rows), F32),
            jax.ShapeDtypeStruct((width, rows), F32),
            jax.ShapeDtypeStruct((1, 2), F32),
        ),
        in_specs=[pl.BlockSpec(memory_space=vmem)] * 3,
        name="normalize",
    )(*(pltpu.with_memory_space_constraint(x, vmem) for x in residuals))
    return mech_out.T, dmg_out.T, norms.reshape(2)


def solution(mesh):
    both = ("dom", "blk")
    in_specs = (
        P(both, None),
        P(both, None),
        P(both, None),
        P(both, None, None, None),
        P(both, None, None, None),
        P(both, None),
        P("dom", None, None),
        P(both, None, None),
        P(both),
        P(),
        P(),
    )
    return jax.shard_map(
        functools.partial(on_device, mesh.shape["dom"], mesh.shape["blk"]),
        mesh=mesh,
        in_specs=in_specs,
        out_specs=(P(both, None), P(both, None), P()),
        check_vma=False,
    )
```

```python
import functools
import math

import jax
import jax.numpy as jnp
from jax import lax
from jax.experimental import pallas as pl
from jax.experimental.pallas import tpu as pltpu
from jax.sharding import PartitionSpec as P

MESH = pl.DeviceIdType.MESH
F32 = jnp.float32
BF16 = jnp.bfloat16
LANES = 128


def dot(a, b):
    return jnp.dot(a, b, preferred_element_type=F32)


def dot_nt(a, b):
    return lax.dot_general(a, b, (((1,), (1,)), ((), ())), preferred_element_type=F32)


def halves(x):
    hi = x.astype(BF16)
    return hi, (x - hi.astype(F32)).astype(BF16)


def as_bf16(mask):
    return jnp.where(mask, 1.0, 0.0).astype(BF16)


def bytes_wait(ref, sem):
    pltpu.make_async_copy(ref, ref, sem).wait()


def block_rows(mat, near, out):
    kblk, width = mat.shape[:2]

    def eight(rb, carry):
        r0 = pl.multiple_of(rb * 8, 8)
        acc = None
        for k in range(kblk):
            for c in range(0, width, 16):
                first = k * width + c
                part = mat[k, pl.ds(r0, 8), c : c + 16, :].astype(F32) * near[first : first + 16, :][None]
                acc = part if acc is None else acc + part
        out[pl.ds(r0, 8), :] = jnp.sum(acc, axis=1)
        return carry

    lax.fori_loop(0, width // 8, eight, 0)


def kernel(
    nd,
    nb,
    disp_h,
    dmg_h,
    load_h,
    tan_h,
    lap_h,
    cols_h,
    lists_h,
    hist_h,
    dest_h,
    smat_h,
    quad_h,
    mech_o,
    dmg_o,
    norm_o,
    disp,
    dmg,
    load,
    tan,
    lap,
    cols,
    lists,
    hist,
    smat,
    quad,
    dall,
    grp_d,
    grp_w,
    pick_d,
    pick_w,
    ghost_d,
    ghost_w,
    pickhot,
    nearhot,
    near_d,
    near_w,
    s_cat,
    diffuse,
    mech,
    ohm,
    h2s,
    h2r,
    h3s,
    h3r,
    ld,
    ss,
    rs,
):
    n = nd * nb
    g1 = 2 * nb
    side = math.isqrt(n // g1)
    width, rows = disp.shape
    kblk = cols.shape[0]
    gmax = lists.shape[1]
    shift = rows.bit_length() - 1
    dom = lax.axis_index("dom")
    blk = lax.axis_index("blk")
    core = lax.rem(dom, 2)
    z, x = dom // (2 * side), lax.rem(dom // 2, side)
    me = dom * nb + blk
    cy = core * nb + blk

    def at(z, x, cy):
        return (z * side + x) * g1 + cy

    def turn(c, step):
        return lax.rem(c + step, side)

    def hops(zx):
        return sum(min(c, side - c) for c in zx)

    far_groups = sorted(((a, b) for a in range(side) for b in range(side)), key=hops, reverse=True)
    far_peers = range(g1 - 1, -1, -1)
    peers_x = [at(z, turn(x, step), cy) for step in range(1, side)]
    peers_z = [at(turn(z, step), x, cy) for step in range(1, side)]
    peers_cy = [at(z, x, jnp.bitwise_xor(cy, step)) for step in range(1, g1)]
    peers_y = [at(z, x, core * nb + lax.rem(blk + step, nb)) for step in range(1, nb)]
    across = lax.rem(jnp.where(core == 0, dom + nd - 1, dom + 1), nd) * nb + blk

    def loc(p):
        return (p // nb, lax.rem(p, nb))

    def send(src, dst, s, r, p):
        pltpu.make_async_remote_copy(
            src_ref=src, dst_ref=dst, send_sem=s, recv_sem=r, device_id=loc(p), device_id_type=MESH
        ).start()

    greeted = [across, *peers_x, *peers_z, *peers_cy]
    loads = []
    for i, (src, dst) in enumerate(
        (
            (dest_h, dall.at[z, x, cy]),
            (dmg_h, dmg),
            (disp_h, disp),
            (lists_h, lists),
            (cols_h, cols),
            (lap_h, lap),
            (smat_h, smat),
            (hist_h, hist),
            (tan_h, tan),
            (load_h, load),
            (quad_h, quad),
        )
    ):
        copy = pltpu.make_async_copy(src, dst, ld.at[i])
        copy.start()
        loads.append(copy)
        if i == 1:
            barrier = pltpu.get_barrier_semaphore()
            for p in greeted:
                pl.semaphore_signal(barrier, inc=1, device_id=loc(p), device_id_type=MESH)
    c_dest, c_dmg, c_disp, c_lists, c_cols, c_lap, c_smat, c_hist, c_tan, c_load, c_quad = loads

    c_dmg.wait()
    damage = dmg[...]
    grp_d[blk] = damage.astype(BF16)
    c_dest.wait()
    pl.semaphore_wait(barrier, len(greeted))

    def spread(part, peers, i):
        for p in peers:
            send(part, part, ss.at[i], rs.at[i], p)

    spread(dall.at[z, x, cy], peers_x, 0)
    spread(grp_d.at[blk], peers_y, 1)

    c_disp.wait()
    root = jnp.sqrt((1.0 - damage) ** 2 + 0.001)
    grp_w[blk] = (root * disp[...]).astype(BF16)
    spread(grp_w.at[blk], peers_y, 3)
    c_lists.wait()
    for which in range(2):
        row = lax.broadcasted_iota(jnp.int32, (nb * rows, gmax), 0)
        pickhot[which] = as_bf16(row == lists[which : which + 1, :])

    bytes_wait(dall.at[0, pl.ds(0, side - 1), 0], rs.at[0])
    spread(dall.at[z, :, cy], peers_z, 2)

    def pick(grp, out, ghost, i):
        for which in range(2):
            total = None
            for b in range(nb):
                part = dot(grp[b], pickhot[which, b * rows : (b + 1) * rows, :])
                total = part if total is None else total + part
            out[which] = total.astype(BF16)

        @pl.when(dom > 0)
        def _():
            send(out.at[0], ghost.at[1], ss.at[i], rs.at[i + 1], me - nb)

        @pl.when(dom < nd - 1)
        def _():
            send(out.at[1], ghost.at[0], ss.at[i + 1], rs.at[i], me + nb)

    bytes_wait(grp_d.at[pl.ds(0, nb - 1)], rs.at[1])
    pick(grp_d, pick_d, ghost_d, 4)

    def near_own(grp, near):
        total = None
        for b in range(nb):
            part = dot(grp[b], nearhot[b * rows : (b + 1) * rows, :])
            total = part if total is None else total + part
        for k in range(kblk):
            near[k * width : (k + 1) * width, :] = total[:, k * rows : (k + 1) * rows]

    c_cols.wait()
    for k in range(kblk):
        entry = lax.broadcasted_iota(jnp.int32, (nearhot.shape[0], rows), 0)
        nearhot[:, k * rows : (k + 1) * rows] = as_bf16(entry == cols[k : k + 1, :])
    before = as_bf16(
        lax.broadcasted_iota(jnp.int32, (rows, rows), 0) < lax.broadcasted_iota(jnp.int32, (rows, rows), 1)
    )
    mine = dall[z, x, cy]
    sent = lax.broadcasted_iota(jnp.int32, (n, rows), 0) == jnp.right_shift(mine, shift)
    rank = dot(as_bf16(sent), before)
    for r in range(2):
        ohm[r] = as_bf16(sent & (rank == r))

    near_own(grp_d, near_d)
    bytes_wait(grp_w.at[pl.ds(0, nb - 1)], rs.at[3])
    pick(grp_w, pick_w, ghost_w, 6)

    bytes_wait(dall.at[pl.ds(0, side - 1), :, 0], rs.at[2])
    spread(dall.at[:, :, cy], peers_cy, 8)

    def ghosts(ghost, i):
        for which, there in ((0, dom > 0), (1, dom < nd - 1)):

            @pl.when(there)
            def _():
                bytes_wait(ghost.at[which], rs.at[i + which])

            @pl.when(jnp.logical_not(there))
            def _():
                ghost[which] = jnp.zeros(ghost.shape[1:], BF16)

    def near_ghosts(ghost, near):
        total = None
        for which in range(2):
            first = nb * rows + which * gmax
            part = dot(ghost[which], nearhot[first : first + gmax, :])
            total = part if total is None else total + part
        for k in range(kblk):
            near[k * width : (k + 1) * width, :] += total[:, k * rows : (k + 1) * rows]

    ghosts(ghost_d, 4)
    near_ghosts(ghost_d, near_d)
    c_lap.wait()
    block_rows(lap, near_d, diffuse)

    bytes_wait(dall.at[:, :, pl.ds(0, g1 - 1)], rs.at[8])
    dest = dall[:, :, :, 0, :].reshape(n, rows)
    wanted = jnp.right_shift(dest, shift) == me
    slot = jnp.bitwise_and(dest, rows - 1).astype(F32)
    order = dot(as_bf16(wanted), before)
    lane = lax.broadcasted_iota(jnp.int32, (n, rows), 1).astype(F32)
    own = []
    for r in range(2):
        held = jnp.sum(jnp.where(wanted & (order == r), slot + 1.0, 0.0), axis=1, keepdims=True)
        own.append(as_bf16(lane + 1.0 == held))

    fields = jnp.concatenate([disp[...], diffuse[...], dmg[...]], axis=0)
    f_hi, f_lo = halves(fields)
    both = jnp.concatenate(own, axis=1)
    void = jnp.zeros(f_hi.shape, BF16)

    def twice(f):
        top = jnp.concatenate([f, void], axis=1)
        low = jnp.concatenate([void, f], axis=1)
        return jnp.concatenate([top, low], axis=0)

    h2s[:, 0, : 6 * width] = dot_nt(both, twice(f_hi)) + dot_nt(both, twice(f_lo))

    def exchange(src, dst, i):
        pltpu.make_async_copy(src.at[me], dst.at[me], rs.at[i]).start()
        for group in far_groups:
            first = at(turn(z, group[0]), turn(x, group[1]), 0)
            for low in far_peers:
                if any(group) or low:
                    p = first + jnp.bitwise_xor(cy, low)
                    send(src.at[p], dst.at[me], ss.at[i], rs.at[i], p)

    exchange(h2s, h2r, 9)

    near_own(grp_w, near_w)
    ghosts(ghost_w, 6)
    near_ghosts(ghost_w, near_w)
    c_tan.wait()
    block_rows(tan, near_w, mech)
    c_load.wait()
    damage = dmg[...]
    root = jnp.sqrt((1.0 - damage) ** 2 + 0.001)
    mech_res = root * mech[...] - load[...]
    mech[...] = mech_res
    mech_part = jnp.sum(mech_res * mech_res)

    c_hist.wait()
    c_quad.wait()
    c_smat.wait()

    @pl.loop(0, smat.shape[0])
    def _(q):
        hi, lo = halves(smat[q])
        gap = jnp.zeros((width, LANES - width), BF16)
        s_cat[q] = jnp.concatenate([hi, gap, lo, gap], axis=1)

    bytes_wait(h2r, rs.at[9])
    g_hi, g_lo = halves(jnp.transpose(h2r[:, 0, : 6 * width]))
    got = None
    for r in range(2):
        rows_r = slice(r * 3 * width, (r + 1) * 3 * width)
        part = dot(g_hi[rows_r], ohm[r]) + dot(g_lo[rows_r], ohm[r])
        got = part if got is None else got + part
    u_hi, u_lo = halves(got[:width])
    u_cat = jnp.concatenate([u_hi, u_lo], axis=1)
    gap = jnp.zeros((LANES - width, 2 * rows), BF16)
    u_cat = jnp.concatenate([u_cat, gap, u_cat, gap], axis=0)

    def points(q, source):
        st = dot(s_cat[q], u_cat)
        st = st[:, :rows] + st[:, rows:]
        return source + quad[q] * jnp.maximum(hist[q], 0.5 * st * st)

    source = lax.fori_loop(0, smat.shape[0], points, jnp.zeros((width, rows), F32), unroll=True)
    there = got[2 * width :]
    dmg_res = got[width : 2 * width] + (1.0 + 2.0 * source) * there - 2.0 * source
    dmg_part = jnp.sum(dmg_res * dmg_res)

    pad = jnp.concatenate([dmg_res, jnp.zeros((LANES - width, rows), F32)], axis=0)
    p_hi, p_lo = halves(pad)
    lane = lax.broadcasted_iota(jnp.int32, (n, LANES), 1)
    for r in range(2):
        back = dot_nt(ohm[r], p_hi) + dot_nt(ohm[r], p_lo)
        if r == 0:
            back = jnp.where(lane == width, mech_part, jnp.where(lane == width + 1, dmg_part, back))
        h3s[:, 0, r * LANES : (r + 1) * LANES] = back
    exchange(h3s, h3r, 10)

    bytes_wait(h3r, rs.at[10])
    first = h3r[:, 0, :LANES]
    total = None
    for r in range(2):
        g_hi, g_lo = halves(jnp.transpose(h3r[:, 0, r * LANES : r * LANES + width]))
        part = dot(g_hi, own[r]) + dot(g_lo, own[r])
        total = part if total is None else total + part
    entries = n * rows * width
    sums = jnp.sum(first, axis=0, keepdims=True)
    norms = jnp.sqrt(sums * (1.0 / entries) + 1e-06)
    mech_o[...] = mech[...]
    dmg_o[...] = total
    norm_o[...] = norms[:, width : width + 2]

    bytes_wait(dall.at[0, pl.ds(0, side - 1), 0], ss.at[0])
    bytes_wait(grp_d.at[pl.ds(0, nb - 1)], ss.at[1])
    bytes_wait(dall.at[pl.ds(0, side - 1), :, 0], ss.at[2])
    bytes_wait(grp_w.at[pl.ds(0, nb - 1)], ss.at[3])
    for i, ghost in ((4, ghost_d), (6, ghost_w)):

        @pl.when(dom > 0)
        def _():
            bytes_wait(ghost.at[0], ss.at[i])

        @pl.when(dom < nd - 1)
        def _():
            bytes_wait(ghost.at[1], ss.at[i + 1])

    bytes_wait(dall.at[:, :, pl.ds(0, g1 - 1)], ss.at[8])
    bytes_wait(h2s.at[pl.ds(0, n - 1)], ss.at[9])
    bytes_wait(h3s.at[pl.ds(0, n - 1)], ss.at[10])


def normalize(mech, dmg, norm, mech_o, dmg_o, norm_o):
    norms = norm[...]
    mech_o[...] = mech[...] / norms[:, 0:1]
    dmg_o[...] = dmg[...] / norms[:, 1:2]
    norm_o[...] = norms


def on_device(
    nd,
    nb,
    displacement,
    damage,
    applied_load,
    tangent,
    laplacian,
    block_columns,
    send_lists,
    hist_mech,
    mech_dest,
    strain_matrix,
    quad_weight,
):
    n = nd * nb
    rows, width = displacement.shape
    kblk = block_columns.shape[1]
    points = hist_mech.shape[1]
    gmax = send_lists.shape[2]
    wl = -(-6 * width // LANES) * LANES
    side = math.isqrt(nd // 2)
    args = (
        displacement.T,
        damage.T,
        applied_load.T,
        jnp.transpose(tangent, (1, 2, 3, 0)),
        jnp.transpose(laplacian, (1, 2, 3, 0)),
        block_columns.T,
        send_lists[0],
        jnp.transpose(hist_mech, (1, 2, 0)),
        mech_dest.reshape(1, rows),
        strain_matrix,
        quad_weight,
    )
    vmem = pltpu.VMEM
    residuals = pl.pallas_call(
        functools.partial(kernel, nd, nb),
        out_shape=(vmem((width, rows), F32), vmem((width, rows), F32), vmem((1, 2), F32)),
        in_specs=[pl.BlockSpec(memory_space=pl.ANY)] * len(args),
        out_specs=[pl.BlockSpec(memory_space=vmem)] * 3,
        scratch_shapes=[
            vmem((width, rows), F32),
            vmem((width, rows), F32),
            vmem((width, rows), F32),
            vmem((kblk, width, width, rows), BF16),
            vmem((kblk, width, width, rows), BF16),
            vmem((kblk, rows), jnp.int32),
            vmem((2, gmax), jnp.int32),
            vmem((points, width, rows), F32),
            vmem((points, width, width), F32),
            pltpu.SMEM((points,), F32),
            vmem((side, side, 2 * nb, 1, rows), jnp.int32),
            vmem((nb, width, rows), BF16),
            vmem((nb, width, rows), BF16),
            vmem((2, width, gmax), BF16),
            vmem((2, width, gmax), BF16),
            vmem((2, width, gmax), BF16),
            vmem((2, width, gmax), BF16),
            vmem((2, nb * rows, gmax), BF16),
            vmem((nb * rows + 2 * gmax, kblk * rows), BF16),
            vmem((kblk * width, rows), F32),
            vmem((kblk * width, rows), F32),
            vmem((points, width, 2 * LANES), BF16),
            vmem((width, rows), F32),
            vmem((width, rows), F32),
            vmem((2, n, rows), BF16),
            vmem((n, 1, wl), F32),
            vmem((n, 1, wl), F32),
            vmem((n, 1, 2 * LANES), F32),
            vmem((n, 1, 2 * LANES), F32),
            pltpu.SemaphoreType.DMA((11,)),
            pltpu.SemaphoreType.DMA((11,)),
            pltpu.SemaphoreType.DMA((11,)),
        ],
        compiler_params=pltpu.CompilerParams(
            collective_id=0, has_side_effects=True, vmem_limit_bytes=60 << 20
        ),
        name="fracture_pass",
    )(*args)
    mech_out, dmg_out, norms = pl.pallas_call(
        normalize,
        out_shape=(
            jax.ShapeDtypeStruct((width, rows), F32),
            jax.ShapeDtypeStruct((width, rows), F32),
            jax.ShapeDtypeStruct((1, 2), F32),
        ),
        in_specs=[pl.BlockSpec(memory_space=vmem)] * 3,
        name="normalize",
    )(*(pltpu.with_memory_space_constraint(x, vmem) for x in residuals))
    return mech_out.T, dmg_out.T, norms.reshape(2)


def solution(mesh):
    both = ("dom", "blk")
    in_specs = (
        P(both, None),
        P(both, None),
        P(both, None),
        P(both, None, None, None),
        P(both, None, None, None),
        P(both, None),
        P("dom", None, None),
        P(both, None, None),
        P(both),
        P(),
        P(),
    )
    return jax.shard_map(
        functools.partial(on_device, mesh.shape["dom"], mesh.shape["blk"]),
        mesh=mesh,
        in_specs=in_specs,
        out_specs=(P(both, None), P(both, None), P()),
        check_vma=False,
    )
```
